32 devices in a mesh: dp: 4 (over y, x), cam: 8 (over z, core).
Axes of the slice: x: 2, y: 2, z: 4, core: 2. Of those that a mesh axis runs over, the one named last changes fastest.
Arguments:
- grad_out: bfloat16 [4096, 3072], P(('dp', 'cam')), may hold values from -6 to 6
- query_act: bfloat16 [4096, 2048], P(('dp', 'cam')), may hold values from -13 to 13
- key_act: bfloat16 [4096, 2048], P(('dp', 'cam')), may hold values from -13 to 13
- value_act: bfloat16 [4096, 2048], P(('dp', 'cam')), may hold values from -6 to 6
- out_proj: bfloat16 [3072, 2048], P('dp'), may hold values from -0.125 to 0.125
- view_counts: int32 [4, 4], P('dp'), may hold values from 1 to 12, 16 in all within a row
- view_slots: int32 [4, 16], P('dp'), may hold values from 0 to 15, each once within a row
Outputs:
- grad_query: bfloat16 [4096, 2048], P(('dp', 'cam'))
- grad_key: bfloat16 [4096, 2048], P(('dp', 'cam'))
- grad_value: bfloat16 [4096, 2048], P(('dp', 'cam'))
- grad_proj: float32 [3072, 2048], P('dp')
The draws below stay inside these ranges and needn't reach their ends.
Inputs may be any that keep to these rules, and one draw needn't show every extreme that they name: `view_counts`: in each group the 4 counts sum to 16, and the largest is exactly 12. `view_slots`: each row is a permutation of the group's 16 slots.
All inputs are finite; a program needn't handle non-finite values.
Results may differ from the reference program's by a relative error of at most 0.0096.
Values may be sent and summed in bfloat16 or wider, within the bound.
No kernel may reach another device: no remote copies, remote signals or barrier semaphores. Data moves between devices by JAX's collectives and lax.ppermute only.
A program may use at most 64 MiB of HBM per device.

```python
import math
import jax
import jax.numpy as jnp
import numpy as np
from jax import lax

D = 3072
HEADS = 16
HEAD_DIM = 128
VIEW_TOK = 64
HD = 2048
GROUP = 16
OBJ = 4
MAXV = 12
TOKENS = 4096
N_DP = 4


def paired_rows(key):
    query_seed = jax.random.fold_in(key, 101)
    key_seed = jax.random.fold_in(key, 202)
    query_rows = jnp.clip(jax.random.normal(query_seed, (TOKENS, HD), jnp.float32), -4.0, 4.0)
    key_rows = jnp.clip(jax.random.normal(key_seed, (TOKENS, HD), jnp.float32), -4.0, 4.0)
    return (query_rows, key_rows)


def draw_query_act(key, part):
    return paired_rows(key)[0].astype(jnp.bfloat16)


def draw_key_act(key, part):
    return paired_rows(key)[1].astype(jnp.bfloat16)


def block_levels(rng, shape, cuts, smallest, high):
    gain = 1.0
    for dim, blocks in cuts:
        steps = jax.random.uniform(jax.random.fold_in(jax.random.fold_in(rng, 6), dim), (blocks,), jnp.float32, smallest / len(cuts), high / len(cuts))
        gain = gain * jnp.repeat(jnp.exp(steps), shape[dim] // blocks).reshape((-1,) + (1,) * (len(shape) - 1 - dim))
    return gain


def profile(number_of, total, most, lean):
    portions = [(1 << 20) // math.isqrt(grade ** lean) + 1 for grade in range(2, number_of + 1)]
    spare, holding = total - most - (number_of - 1), [1] * (number_of - 1)
    while spare > 0:
        movable = [i for i in range(number_of - 1) if holding[i] < most]
        pool, budget = sum([portions[i] for i in movable]), spare
        for i in movable:
            extra = min(most - holding[i], max(1, budget * portions[i] // pool), spare)
            holding[i] = holding[i] + extra
            spare = spare - extra
    return np.array([most] + holding)


def ragged_sizes(key, number_of, total, most, slope):
    if number_of == 2:
        one = jax.random.randint(key, (), max(1, total - most), min(most, total - 1) + 1)
        return jnp.stack([one, total - one])
    tallies = jnp.asarray(profile(number_of, total, most, slope), jnp.int32)
    couples = (number_of - 1) // 2
    donor, sink = tallies[1:1 + 2 * couples:2], tallies[2:2 + 2 * couples:2]
    room = jnp.minimum(donor - 1, most - sink)
    moved = jax.random.randint(jax.random.fold_in(key, 1), (couples,), 0, 1 << 20) % (room + 1)
    tallies = tallies.at[1:1 + 2 * couples:2].set(donor - moved).at[2:2 + 2 * couples:2].set(sink + moved)
    return tallies[jax.random.permutation(jax.random.fold_in(key, 2), number_of)]


def normal_values(stream_key, extent, width, most, cuts=(), held_as=jnp.bfloat16):
    factor_of = block_levels(stream_key, extent, cuts, -0.22, 0.18) if cuts else 1.0
    drawn = jax.random.normal(stream_key, extent, jnp.float32) * width * factor_of
    return jnp.minimum(jnp.maximum(drawn, -most), most).astype(held_as)


def setup_inputs(seed: int = 0) -> dict:
    arg_keys = jax.random.split(jax.random.key(seed), 8)
    return {
        "grad_out": normal_values(arg_keys[0], (TOKENS, D), 1.0, 6.0, ((0, 32),)),
        "query_act": draw_query_act(jax.random.fold_in(arg_keys[7], 71), 0),
        "key_act": draw_key_act(jax.random.fold_in(arg_keys[7], 71), 0),
        "value_act": normal_values(arg_keys[3], (TOKENS, HD), 1.0, 6.0, ((0, 32),)),
        "out_proj": normal_values(arg_keys[4], (D, HD), HD ** -0.5, 0.125, ((0, 4),)),
        "view_counts": jax.vmap(lambda own: ragged_sizes(own, OBJ, GROUP, MAXV, 2))(jax.random.split(arg_keys[5], N_DP)).reshape((N_DP, OBJ)).astype(jnp.int32),
        "view_slots": jax.vmap(lambda own: jax.random.permutation(own, GROUP))(jax.random.split(arg_keys[6], N_DP)).reshape((N_DP, GROUP)).astype(jnp.int32),
    }


def token_objects(counts, slots, view_tokens):
    count_ends = jnp.cumsum(counts).astype(jnp.int32)
    view_order = jnp.arange(slots.shape[0], dtype=jnp.int32)
    view_object = lax.optimization_barrier(jnp.sum((view_order[:, None] >= count_ends[None, :]).astype(jnp.int32), axis=1)).astype(jnp.int32)
    placed = slots[:, None] == view_order[None, :]
    slot_object = lax.optimization_barrier(jnp.sum(jnp.where(placed, view_object[:, None], 0), axis=0)).astype(jnp.int32)
    return jnp.repeat(slot_object, view_tokens)

def group_attention(query_group, key_group, value_group, grad_group, same_object):
    group_tokens = query_group.shape[0]
    score_scale = 1.0 / math.sqrt(HEAD_DIM)
    query_split = query_group.astype(jnp.float32).reshape(group_tokens, HEADS, HEAD_DIM)
    key_split = key_group.astype(jnp.float32).reshape(group_tokens, HEADS, HEAD_DIM)
    value_split = value_group.astype(jnp.float32).reshape(group_tokens, HEADS, HEAD_DIM)
    grad_split = grad_group.astype(jnp.float32).reshape(group_tokens, HEADS, HEAD_DIM)
    scores = jnp.einsum('qhd,khd->hqk', query_split, key_split) * score_scale
    scores = jnp.where(same_object[None, :, :], scores, -jnp.inf)
    row_max = lax.optimization_barrier(jnp.max(scores, axis=2, keepdims=True))
    exp_scores = jnp.exp(scores - row_max)
    probs = exp_scores / lax.optimization_barrier(jnp.sum(exp_scores, axis=2, keepdims=True))
    probs_bf16 = probs.astype(jnp.bfloat16)
    probs_wide = probs_bf16.astype(jnp.float32)
    attended_f32 = jnp.einsum('hqk,khd->qhd', probs_wide, value_split)
    row_delta = lax.optimization_barrier(jnp.sum(grad_split * attended_f32, axis=2))
    grad_probs = jnp.einsum('qhd,khd->hqk', grad_split, value_split)
    grad_scores = (probs * (grad_probs - jnp.transpose(row_delta)[:, :, None])).astype(jnp.bfloat16)
    grad_wide = grad_scores.astype(jnp.float32)
    grad_query = jnp.einsum('hqk,khd->qhd', grad_wide, key_split) * score_scale
    grad_key = jnp.einsum('hqk,qhd->khd', grad_wide, query_split) * score_scale
    grad_value = jnp.einsum('hqk,qhd->khd', probs_wide, grad_split)
    shape_flat = (group_tokens, HEADS * HEAD_DIM)
    return (attended_f32.reshape(shape_flat).astype(jnp.bfloat16), grad_query.reshape(shape_flat).astype(jnp.bfloat16), grad_key.reshape(shape_flat).astype(jnp.bfloat16), grad_value.reshape(shape_flat).astype(jnp.bfloat16))

def reference(grad_out, query_act, key_act, value_act, out_proj, view_counts, view_slots):
    grad_attn = jnp.dot(grad_out, out_proj, preferred_element_type=jnp.float32).astype(jnp.bfloat16)
    group_count = view_counts.shape[0]
    group_tokens = GROUP * VIEW_TOK

    def one_group(group_index):
        first_row = (group_index * group_tokens).astype(jnp.int32)
        query_group = lax.dynamic_slice_in_dim(query_act, first_row, group_tokens, 0)
        key_group = lax.dynamic_slice_in_dim(key_act, first_row, group_tokens, 0)
        value_group = lax.dynamic_slice_in_dim(value_act, first_row, group_tokens, 0)
        grad_group = lax.dynamic_slice_in_dim(grad_attn, first_row, group_tokens, 0)
        objects = token_objects(view_counts[group_index], view_slots[group_index], VIEW_TOK)
        same_object = objects[:, None] == objects[None, :]
        return group_attention(query_group, key_group, value_group, grad_group, same_object)
    attended, grad_query, grad_key, grad_value = lax.map(one_group, jnp.arange(group_count, dtype=jnp.int32))
    attended = attended.reshape(TOKENS, HD)
    grad_query = grad_query.reshape(TOKENS, HD)
    grad_key = grad_key.reshape(TOKENS, HD)
    grad_value = grad_value.reshape(TOKENS, HD)
    grad_proj = lax.dot_general(grad_out, attended, (((0,), (0,)), ((), ())), preferred_element_type=jnp.float32)
    return (grad_query, grad_key, grad_value, grad_proj)
```

```python
import functools
import math

import jax
import jax.numpy as jnp
from jax import lax
from jax.experimental import pallas as pl
from jax.experimental.pallas import tpu as pltpu
from jax.sharding import PartitionSpec as P

HEAD_DIM = 128
VIEW_TOK = 64
MAXV = 12
LANES = 128
COL_BLOCK = 256


BF16 = jnp.bfloat16
F32 = jnp.float32


def dot_nt(a, b):
    return lax.dot_general(a, b, (((1,), (1,)), ((), ())), preferred_element_type=F32)


def dot_tn(a, b):
    return lax.dot_general(a, b, (((0,), (0,)), ((), ())), preferred_element_type=F32)


def dot_nn(a, b):
    return jnp.dot(a, b, preferred_element_type=F32)


def whole_call(body, out_shape, scalars=0, arrays=0, scratch=(), name=None):
    in_specs = [pl.BlockSpec(memory_space=pltpu.SMEM)] * scalars
    in_specs += [pl.BlockSpec(memory_space=pltpu.VMEM)] * arrays
    out_specs = [pl.BlockSpec(memory_space=pltpu.VMEM)] * len(out_shape)
    return pl.pallas_call(
        body,
        out_shape=tuple(out_shape),
        in_specs=in_specs,
        out_specs=tuple(out_specs),
        scratch_shapes=list(scratch),
        name=name,
    )


def shape_of(shape, dtype):
    return jax.ShapeDtypeStruct(shape, dtype)


def pack_grad_kernel(dp_n, g_ref, mine_ref, other_ref):
    dp, core = lax.axis_index("dp"), lax.rem(lax.axis_index("cam"), 2)
    half = g_ref.shape[1] // dp_n // 2
    for s in range(dp_n):
        base = lax.bitwise_xor(dp, jnp.int32(s)) * (2 * half)
        cols = slice(s * half, (s + 1) * half)
        mine_ref[:, cols] = g_ref[:, pl.ds(pl.multiple_of(base + core * half, LANES), half)]
        other_ref[:, cols] = g_ref[:, pl.ds(pl.multiple_of(base + (1 - core) * half, LANES), half)]


def pack_heads_kernel(cam_n, q_ref, k_ref, v_ref, *out_refs):
    cam = lax.axis_index("cam")
    width = q_ref.shape[1] // cam_n
    for s in range(cam_n):
        first = pl.multiple_of(lax.bitwise_xor(cam, jnp.int32(s)) * width, LANES)
        for t, ref in enumerate((q_ref, k_ref, v_ref)):
            out_refs[s][t] = ref[:, pl.ds(first, width)]


def pack_weight_kernel(cam_n, w_ref, out_ref):
    cam = lax.axis_index("cam")
    core = lax.rem(cam, 2)
    half = w_ref.shape[0] // 2
    width = w_ref.shape[1] // cam_n
    rows = pl.ds(pl.multiple_of(core * half, 16), half)
    other = lax.bitwise_xor(cam, jnp.int32(1))
    out_ref[:, :width] = w_ref[rows, pl.ds(pl.multiple_of(cam * width, LANES), width)]
    out_ref[:, width:] = w_ref[rows, pl.ds(pl.multiple_of(other * width, LANES), width)]


def place_views(counts_ref, slots_ref, pos_ref, slot_ref, object_ref):
    objects, views = counts_ref.shape[1], slots_ref.shape[1]
    ends, total, big = [], jnp.int32(0), jnp.int32(0)
    for o in range(objects):
        count = counts_ref[0, o]
        big = jnp.where(count == MAXV, total, big)
        total = total + count
        ends.append(total)
    for v in range(views):
        pos = jnp.where(v < big, MAXV + v, jnp.where(v < big + MAXV, v - big, v))
        slot = slots_ref[0, v]
        pos_ref[slot] = pos
        slot_ref[pos] = slot
        object_ref[pos] = sum((v >= e).astype(jnp.int32) for e in ends)


def tail_mask(object_ref, views):
    tail = views - MAXV
    size = tail * VIEW_TOK

    def objects(axis):
        view = lax.broadcasted_iota(jnp.int32, (size, size), axis) // VIEW_TOK
        held = jnp.full((size, size), object_ref[MAXV], jnp.int32)
        for i in range(1, tail):
            held = jnp.where(view == i, object_ref[MAXV + i], held)
        return held

    return objects(0) == objects(1)


def blocks_of(tokens):
    big = MAXV * VIEW_TOK
    return ((0, big, False), (big, tokens - big, True))


def attend_kernel(cam_n, counts_ref, slots_ref, *refs):
    x_refs = refs[:cam_n]
    att_ref, xs_ref, att_t_ref, big_ref, tail_ref = refs[cam_n : cam_n + 5]
    pos_ref, slot_ref, object_ref = refs[cam_n + 5 :]
    cam = lax.axis_index("cam")
    rows, width = x_refs[0].shape[1:]
    tokens, views = rows * cam_n, slots_ref.shape[1]
    per_device = rows // VIEW_TOK
    scale = 1.0 / math.sqrt(HEAD_DIM)
    place_views(counts_ref, slots_ref, pos_ref, slot_ref, object_ref)
    for s in range(cam_n):
        first = lax.bitwise_xor(cam, jnp.int32(s)) * per_device
        for i in range(per_device):
            to = pl.ds(pl.multiple_of(pos_ref[first + i] * VIEW_TOK, VIEW_TOK), VIEW_TOK)
            for t in range(3):
                xs_ref[t, to, :] = x_refs[s][t, i * VIEW_TOK : (i + 1) * VIEW_TOK, :]
    same = tail_mask(object_ref, views)
    for head in range(width // HEAD_DIM):
        cols = slice(head * HEAD_DIM, (head + 1) * HEAD_DIM)
        for start, size, masked in blocks_of(tokens):
            keys = xs_ref[1, start : start + size, cols]
            values_t = xs_ref[2, start : start + size, cols].T
            p_ref = tail_ref if masked else big_ref
            step = min(COL_BLOCK, size)
            for c in range(0, size, step):
                scores = dot_nt(keys, xs_ref[0, start + c : start + c + step, cols]) * scale
                if masked:
                    scores = jnp.where(same[:, c : c + step], scores, -jnp.inf)
                e = jnp.exp(scores - jnp.max(scores, axis=0, keepdims=True))
                p = (e * (1.0 / jnp.sum(e, axis=0, keepdims=True))).astype(BF16)
                p_ref[head, :, c : c + step] = p
                att_t = dot_nn(values_t, p)
                att_t_ref[head, :, start + c : start + c + step] = att_t
                att = att_t.T.astype(BF16)
                for i in range(step // VIEW_TOK):
                    slot = slot_ref[(start + c) // VIEW_TOK + i]
                    to = pl.ds(pl.multiple_of(slot * VIEW_TOK, VIEW_TOK), VIEW_TOK)
                    att_ref[to, cols] = att[i * VIEW_TOK : (i + 1) * VIEW_TOK, :]


def grad_attn_kernel(chunks, *refs):
    g_refs, w_refs = refs[:chunks], refs[chunks:-2]
    own_ref, send_ref = refs[-2:]
    rows, width = own_ref.shape[1:]
    weight = jnp.concatenate([w[...] for w in w_refs], axis=0)
    for i in range(0, chunks, 2):
        lhs = jnp.concatenate([g_refs[i][...], g_refs[i + 1][...]], axis=0)
        out = dot_nn(lhs, weight)
        for k in range(2):
            own_ref[i + k] = out[k * rows : (k + 1) * rows, :width]
            send_ref[i + k] = out[k * rows : (k + 1) * rows, width:].astype(BF16)


def backward_kernel(cam_n, counts_ref, slots_ref, *refs):
    early_ref, early_got_ref, late_ref, late_got_ref = refs[:4]
    xs_ref, att_t_ref, big_ref, tail_ref = refs[4:8]
    y_refs = refs[8 : 8 + cam_n]
    g_ref, ds_ref, y_ref, pos_ref, slot_ref, object_ref = refs[8 + cam_n :]
    cam = lax.axis_index("cam")
    chip, core, chips = cam // 2, lax.rem(cam, 2), cam_n // 2
    rows, width = early_ref.shape[1:]
    tokens = rows * cam_n
    per_device = rows // VIEW_TOK
    scale = 1.0 / math.sqrt(HEAD_DIM)
    place_views(counts_ref, slots_ref, pos_ref, slot_ref, object_ref)

    def chunk(step, way, early, late):
        i = 2 * step + way
        return early[i] if step < chips - 1 else late[i - 2 * (chips - 1)]

    for step in range(chips):
        back = (chips - step) % chips
        for way in range(2):
            total = chunk(step, way, early_ref, late_ref) + chunk(
                back, 1 - way, early_got_ref, late_got_ref
            ).astype(F32)
            total = total.astype(BF16)
            if way == 0:
                source = lax.rem(chip - step + chips, chips) * 2 + core
            else:
                source = lax.rem(chip + step, chips) * 2 + 1 - core
            for i in range(per_device):
                pos = pos_ref[source * per_device + i]
                to = pl.ds(pl.multiple_of(pos * VIEW_TOK, VIEW_TOK), VIEW_TOK)
                g_ref[to, :] = total[i * VIEW_TOK : (i + 1) * VIEW_TOK, :]

    def put(t, start, block, cols):
        for i in range(block.shape[0] // VIEW_TOK):
            slot = slot_ref[start // VIEW_TOK + i]
            to = pl.ds(pl.multiple_of(slot * VIEW_TOK, VIEW_TOK), VIEW_TOK)
            y_ref[t, to, cols] = block[i * VIEW_TOK : (i + 1) * VIEW_TOK, :]

    for head in range(width // HEAD_DIM):
        cols = slice(head * HEAD_DIM, (head + 1) * HEAD_DIM)
        for start, size, masked in blocks_of(tokens):
            at = slice(start, start + size)
            values = xs_ref[2, at, cols]
            keys_t = xs_ref[1, at, cols].T
            grads = g_ref[at, cols]
            p_ref = tail_ref if masked else big_ref
            grads_t = grads.astype(F32).T
            delta = jnp.sum(grads_t * att_t_ref[head, :, at], axis=0, keepdims=True)
            step = min(COL_BLOCK, size)
            for c in range(0, size, step):
                grad_p = dot_nt(values, g_ref[start + c : start + c + step, cols])
                p = p_ref[head, :, c : c + step].astype(F32)
                ds = (p * (grad_p - delta[:, c : c + step])).astype(BF16)
                ds_ref[:size, c : c + step] = ds
                grad_q = (dot_nn(keys_t, ds) * scale).T
                put(0, start + c, grad_q.astype(BF16), cols)
            grad_k = dot_nn(ds_ref[:size, :size], xs_ref[0, at, cols]) * scale
            put(1, start, grad_k.astype(BF16), cols)
            put(2, start, dot_nn(p_ref[head], grads).astype(BF16), cols)
    for s in range(cam_n):
        first = lax.bitwise_xor(cam, jnp.int32(s)) * rows
        for t in range(3):
            y_refs[s][t] = y_ref[t, pl.ds(pl.multiple_of(first, rows), rows), :]


def grad_proj_kernel(dp_n, chips, *refs):
    g_refs, (mine_ref, other_ref), out_refs = (
        refs[: 2 * chips],
        refs[2 * chips : 2 * chips + 2],
        refs[2 * chips + 2 :],
    )
    cam = lax.axis_index("cam")
    chip, core = cam // 2, lax.rem(cam, 2)
    rows = g_refs[0].shape[0]
    half = g_refs[0].shape[1] // dp_n
    low, high = [], []
    for step in range(chips):
        for way in range(2):
            if way == 0:
                source = lax.rem(chip - step + chips, chips) * 2 + core
            else:
                source = lax.rem(chip + step, chips) * 2 + 1 - core
            at = pl.ds(pl.multiple_of(source * rows, rows), rows)
            mine, other = mine_ref[at, :], other_ref[at, :]
            low.append(jnp.where(core == 0, mine, other))
            high.append(jnp.where(core == 0, other, mine))
    attended = jnp.concatenate(
        [jnp.concatenate(low, axis=0), jnp.concatenate(high, axis=0)], axis=1
    )
    for s in range(dp_n):
        grads = jnp.concatenate([r[:, s * half : (s + 1) * half] for r in g_refs], axis=0)
        out = dot_tn(grads, attended)
        out_refs[s][...] = out.astype(out_refs[s].dtype)


def unpack_kernel(cam_n, *refs):
    y_refs, out_refs = refs[:cam_n], refs[cam_n:]
    cam = lax.axis_index("cam")
    width = y_refs[0].shape[2]
    for s in range(cam_n):
        first = pl.multiple_of(lax.bitwise_xor(cam, jnp.int32(s)) * width, LANES)
        for t in range(3):
            out_refs[t][:, pl.ds(first, width)] = y_refs[s][t]


def fast(grad_out, query_act, key_act, value_act, out_proj, view_counts, view_slots):
    dp_n, cam_n = lax.axis_size("dp"), lax.axis_size("cam")
    chips = cam_n // 2
    cam = lax.axis_index("cam")
    chip, core = cam // 2, lax.rem(cam, 2)
    rows, model = grad_out.shape
    proj = query_act.shape[1]
    width = proj // cam_n
    tokens = rows * cam_n
    half = model // dp_n // 2
    heads = width // HEAD_DIM
    big = MAXV * VIEW_TOK
    small = tokens - big
    views = view_slots.shape[1]

    def ring(way):
        return [
            (z * 2 + c, ((z + way) % chips) * 2 + c) for z in range(chips) for c in range(2)
        ]

    def swap(x):
        return lax.ppermute(x, "cam", [(i, i ^ 1) for i in range(cam_n)])

    def cam_xor(x, s):
        return lax.ppermute(x, "cam", [(i, i ^ s) for i in range(cam_n)])

    def dp_xor(x, s):
        return lax.ppermute(x, "dp", [(i, i ^ s) for i in range(dp_n)])

    view_scratch = [pltpu.SMEM((views,), jnp.int32)] * 3

    mine, other = whole_call(
        functools.partial(pack_grad_kernel, dp_n),
        [shape_of((rows, model // 2), BF16)] * 2,
        arrays=1,
        name="pack_grad",
    )(grad_out)
    packed = whole_call(
        functools.partial(pack_heads_kernel, cam_n),
        [shape_of((3, rows, width), BF16)] * cam_n,
        arrays=3,
        name="pack_heads",
    )(query_act, key_act, value_act)
    (weight,) = whole_call(
        functools.partial(pack_weight_kernel, cam_n),
        [shape_of((half, 2 * width), BF16)],
        arrays=1,
        name="pack_weight",
    )(out_proj)

    with jax.named_scope("swap_grad"):
        forth, back = [mine], [swap(other)]
    with jax.named_scope("heads_in"):
        heads_in = [packed[0]] + [cam_xor(packed[s], s) for s in range(1, cam_n)]
    with jax.named_scope("weights"):
        weights = [weight] + [dp_xor(weight, s) for s in range(1, dp_n)]
    for step in range(1, chips):
        with jax.named_scope(f"ring{step}"):
            forth.append(lax.ppermute(forth[-1], "cam", ring(1)))
            back.append(lax.ppermute(back[-1], "cam", ring(-1)))
    chunks = [x for pair in zip(forth, back) for x in pair]

    attended, sorted_heads, attended_t, probs, tail_probs = whole_call(
        functools.partial(attend_kernel, cam_n),
        [
            shape_of((tokens, width), BF16),
            shape_of((3, tokens, width), BF16),
            shape_of((heads, HEAD_DIM, tokens), F32),
            shape_of((heads, big, big), BF16),
            shape_of((heads, small, small), BF16),
        ],
        scalars=2,
        arrays=cam_n,
        scratch=view_scratch,
        name="attend",
    )(view_counts, view_slots, *heads_in)
    with jax.named_scope("swap_attended"):
        attended_other = swap(attended)

    def grad_attn(parts, name):
        n = len(parts)
        return whole_call(
            functools.partial(grad_attn_kernel, n),
            [shape_of((n, rows, width), F32), shape_of((n, rows, width), BF16)],
            arrays=n + dp_n,
            name=name,
        )(*parts, *weights)

    early, early_send = grad_attn(chunks[:-2], "grad_attn_early")
    with jax.named_scope("swap_early"):
        early_got = swap(early_send)
    late, late_send = grad_attn(chunks[-2:], "grad_attn_late")
    with jax.named_scope("swap_late"):
        late_got = swap(late_send)

    partial = whole_call(
        functools.partial(grad_proj_kernel, dp_n, chips),
        [shape_of((half, 2 * width), F32)] + [shape_of((half, 2 * width), BF16)] * (dp_n - 1),
        arrays=cam_n + 2,
        name="grad_proj",
    )(*chunks, attended, attended_other)
    with jax.named_scope("sum_dp"):
        others = [dp_xor(partial[s], s) for s in range(1, dp_n)]

    results = whole_call(
        functools.partial(backward_kernel, cam_n),
        [shape_of((3, rows, width), BF16)] * cam_n,
        scalars=2,
        arrays=8,
        scratch=[
            pltpu.VMEM((tokens, width), BF16),
            pltpu.VMEM((big, big), BF16),
            pltpu.VMEM((3, tokens, width), BF16),
        ]
        + view_scratch,
        name="backward",
    )(
        view_counts,
        view_slots,
        early,
        early_got,
        late,
        late_got,
        sorted_heads,
        attended_t,
        probs,
        tail_probs,
    )
    with jax.named_scope("heads_out"):
        heads_out = [results[0]] + [cam_xor(results[s], s) for s in range(1, cam_n)]

    total = partial[0]
    for item in others:
        total = total + item.astype(F32)
    total = total.astype(BF16)
    grad_proj = jnp.zeros((2 * half, proj), F32)
    quarter = half // 2

    def place(out, block, which, from_chip, part):
        row = which * half + part * quarter
        return lax.dynamic_update_slice(out, block.astype(F32), (row, from_chip * 2 * width))

    rings = [total[:quarter], total[quarter:]]
    for step in range(chips):
        with jax.named_scope(f"out_ring{step}"):
            for way in range(2):
                if step:
                    rings[way] = lax.ppermute(rings[way], "cam", ring(1 - 2 * way))
                from_chip = lax.rem(chip + (step if way else chips - step), chips)
                partner = swap(rings[way])
                grad_proj = place(grad_proj, rings[way], core, from_chip, way)
                grad_proj = place(grad_proj, partner, 1 - core, from_chip, way)

    grads = whole_call(
        functools.partial(unpack_kernel, cam_n),
        [shape_of((rows, proj), BF16)] * 3,
        arrays=cam_n,
        name="unpack",
    )(*heads_out)
    return (*grads, grad_proj)


def token_objects(counts, slots, view_tokens):
    count_ends = jnp.cumsum(counts)
    view_order = jnp.arange(slots.shape[0], dtype=jnp.int32)
    view_object = jnp.sum((view_order[:, None] >= count_ends[None, :]).astype(jnp.int32), axis=1)
    placed = slots[:, None] == view_order[None, :]
    slot_object = jnp.sum(jnp.where(placed, view_object[:, None], 0), axis=0)
    return jnp.repeat(slot_object, view_tokens)


def head_attention(query_heads, key_heads, value_heads, grad_heads, same_object, head_dim):
    group_tokens, proj_width = query_heads.shape
    head_count = proj_width // head_dim
    score_scale = 1.0 / math.sqrt(head_dim)

    def one_head(head_index):
        first_col = head_index * head_dim
        query_one = lax.dynamic_slice_in_dim(query_heads, first_col, head_dim, 1)
        key_one = lax.dynamic_slice_in_dim(key_heads, first_col, head_dim, 1)
        value_one = lax.dynamic_slice_in_dim(value_heads, first_col, head_dim, 1)
        grad_one = lax.dynamic_slice_in_dim(grad_heads, first_col, head_dim, 1)
        scores = jnp.where(same_object, dot_nt(query_one, key_one) * score_scale, -jnp.inf)
        exp_scores = jnp.exp(scores - jnp.max(scores, axis=1, keepdims=True))
        probs = exp_scores / jnp.sum(exp_scores, axis=1, keepdims=True)
        probs_bf16 = probs.astype(BF16)
        attended_f32 = dot_nn(probs_bf16, value_one)
        row_delta = jnp.sum(grad_one.astype(F32) * attended_f32, axis=1)
        grad_probs = dot_nt(grad_one, value_one)
        grad_scores = (probs * (grad_probs - row_delta[:, None])).astype(BF16)
        grad_query = dot_nn(grad_scores, key_one) * score_scale
        grad_key = dot_tn(grad_scores, query_one) * score_scale
        grad_value = dot_tn(probs_bf16, grad_one)
        return tuple(x.astype(BF16) for x in (attended_f32, grad_query, grad_key, grad_value))

    stacked = lax.map(one_head, jnp.arange(head_count, dtype=jnp.int32))

    def flatten(per_head):
        return jnp.transpose(per_head, (1, 0, 2)).reshape(group_tokens, proj_width)

    return tuple(flatten(item) for item in stacked)


def general(grad_out, query_act, key_act, value_act, out_proj, view_counts, view_slots):
    cam_count = lax.axis_size("cam")
    cam_index = lax.axis_index("cam")
    local_width = query_act.shape[1] // cam_count
    objects = token_objects(view_counts[0], view_slots[0], VIEW_TOK)
    same_object = objects[:, None] == objects[None, :]
    whole_out = lax.all_gather(grad_out, "cam", axis=0, tiled=True)
    own_columns = lax.dynamic_slice_in_dim(out_proj, cam_index * local_width, local_width, 1)
    columns = lax.all_gather(own_columns, "dp", axis=0, tiled=True)
    grad_heads = dot_nn(whole_out, columns).astype(BF16)
    heads = [
        lax.all_to_all(x, "cam", split_axis=1, concat_axis=0, tiled=True)
        for x in (query_act, key_act, value_act)
    ]
    attended, *grads = head_attention(*heads, grad_heads, same_object, HEAD_DIM)
    partial_rows = lax.psum_scatter(
        dot_tn(whole_out, attended), "dp", scatter_dimension=0, tiled=True
    )
    grad_proj = lax.all_gather(partial_rows, "cam", axis=1, tiled=True)
    grads = [lax.all_to_all(x, "cam", split_axis=0, concat_axis=1, tiled=True) for x in grads]
    return (*grads, grad_proj)


def fits(mesh, grad_out, query_act, view_slots):
    dp_n, cam_n = mesh.shape["dp"], mesh.shape["cam"]
    powers = all(n & (n - 1) == 0 for n in (dp_n, cam_n))
    half, rest = divmod(grad_out.shape[1], 2 * dp_n)
    width = query_act.shape[1] // cam_n
    return (
        powers
        and cam_n >= 4
        and rest == 0
        and half % LANES == 0
        and width % HEAD_DIM == 0
        and view_slots.shape[1] - MAXV == 4
    )


def solution(mesh):
    def step(*args):
        grad_out, query_act, view_slots = args[0], args[1], args[6]
        rows, dp_rows = P(("dp", "cam"), None), P("dp", None)
        return jax.shard_map(
            fast if fits(mesh, grad_out, query_act, view_slots) else general,
            mesh=mesh,
            in_specs=(rows, rows, rows, rows, dp_rows, dp_rows, dp_rows),
            out_specs=(rows, rows, rows, dp_rows),
            check_vma=False,
        )(*args)

    return step
```
